32 devices in a mesh: groups: 2 (over x), row: 16 (over z, y, core).
Axes of the slice: x: 2, y: 2, z: 4, core: 2. Of those that a mesh axis runs over, the one named last changes fastest.
Arguments:
- features: bfloat16 [128, 64, 512], P(('groups', 'row')), parts along dimension 0, may hold values from -6 to 6
- cotangent: bfloat16 [128, 64, 512], P(('groups', 'row')), parts along dimension 0, may hold values from -6 to 6
- depth_weight: bfloat16 [49, 512], P(None, 'row'), may hold values from -0.875 to 0.875
- depth_bias: bfloat16 [512], P('row'), may hold values from -3 to 3
- norm_gain: bfloat16 [512], P('row'), may hold values from 0.25 to 1.75
- norm_shift: bfloat16 [512], P('row'), may hold values from -3 to 3
- up_weight: bfloat16 [512, 2048], P('row'), may hold values from -0.25 to 0.25
- up_bias: bfloat16 [2048], P('row'), may hold values from -3 to 3
- down_weight: bfloat16 [2048, 512], P('row'), may hold values from -0.125 to 0.125
- down_bias: bfloat16 [512], P('row'), may hold values from -3 to 3
Outputs:
- block_out: bfloat16 [128, 64, 512], P(('groups', 'row')), parts along dimension 0
- grad_features: bfloat16 [128, 64, 512], P(('groups', 'row')), parts along dimension 0
- grad_up_weight: float32 [1024, 2048], P(('groups', 'row')), parts along dimension 0
- grad_down_weight: float32 [4096, 512], P(('groups', 'row')), parts along dimension 0
- grad_depth_weight: float32 [98, 512], P('groups', 'row'), parts along dimension 0
- grad_depth_bias: float32 [1024], P(('groups', 'row')), parts along dimension 0
- grad_norm_gain: float32 [1024], P(('groups', 'row')), parts along dimension 0
- grad_norm_shift: float32 [1024], P(('groups', 'row')), parts along dimension 0
- grad_up_bias: float32 [4096], P(('groups', 'row')), parts along dimension 0
- grad_down_bias: float32 [1024], P(('groups', 'row')), parts along dimension 0
The draws below stay inside these ranges and needn't reach their ends.
There are 2 independent parts, one for each index of `groups`. The reference program is written for one: setup_inputs(seed, part) draws one part's arguments, and reference() takes and returns one part's arrays. A program takes and returns all parts, laid end to end along the dimension named above; an argument that names none is the same for every part. Nothing has to cross between parts.
All inputs are finite; a program needn't handle non-finite values.
Results may differ from the reference program's by a relative error of at most 0.0055.
Values may be sent and summed in bfloat16 or wider, within the bound.
A program may use at most 64 MiB of HBM per device.

```python
import math
import jax
import jax.numpy as jnp
from jax import lax

C = 512
HID = 2048
COLS = 64
H = 64
TOKENS = 4096


def with_spikes(result, key, source, target, shards_of, factor):
    def block_of(axis_at):
        return (jnp.arange(result.shape[axis_at]) // (result.shape[axis_at] // shards_of)).reshape((-1,) + (1,) * (result.ndim - 1 - axis_at))

    one_side = jax.random.permutation(key, shards_of)[block_of(target)]
    far = (block_of(target) + shards_of // 2) % shards_of
    return jnp.where((block_of(source) == one_side) | (block_of(source) == far), factor * result, result)


def steps_of(own_key, dims, pieces, low, largest):
    level, own = 1.0, jax.random.fold_in(own_key, 6)
    for position, parts in pieces:
        draws = jnp.exp(jax.random.uniform(jax.random.fold_in(own, position), (parts,), jnp.float32, low / len(pieces), largest / len(pieces)))
        level = level * jnp.repeat(draws, dims[position] // parts).reshape([-1 if axis == position else 1 for axis in range(len(dims))])
    return level


def scatter_about(own_key, shape, spread, reach, split=(), kind=jnp.bfloat16):
    entries = jax.random.normal(own_key, shape, jnp.float32) * spread
    if len(split) > 0:
        entries = steps_of(own_key, shape, split, -0.22, 0.18) * entries
    return jnp.clip(entries, min=-reach, max=reach).astype(kind)


def noise_with(stream_key, dims, scale, reach, pieces, heavy, kind=jnp.bfloat16):
    drawn = scale * jax.random.normal(stream_key, dims, jnp.float32)
    if pieces:
        drawn = drawn * steps_of(stream_key, dims, pieces, -0.22, 0.18)
    return jnp.clip(with_spikes(drawn, jax.random.fold_in(stream_key, 3), *heavy), -reach, reach).astype(kind)


def setup_inputs(seed: int = 0, part: int = 0) -> dict:
    key_of = jax.random.split(jax.random.key(seed), 11)
    part_keys = jax.random.split(jax.random.fold_in(key_of[10], part), 11)
    features = noise_with(part_keys[0], (H, COLS, C), 1.0, 6.0, ((0, 16),), (0, 2, 16, 2.0))
    cotangent = noise_with(part_keys[1], (H, COLS, C), 1.0, 6.0, ((0, 16),), (0, 2, 16, 2.0))
    depth_weight = scatter_about(key_of[2], (49, C), 49 ** -0.5, 0.875, ((1, 16),))
    depth_bias = scatter_about(key_of[3], (C,), 0.5, 3.0, ((0, 16),))
    norm_gain = jnp.clip(1.0 + 0.15 * jax.random.normal(key_of[4], (C,), jnp.float32), 0.25, 1.75).astype(jnp.bfloat16)
    norm_shift = scatter_about(key_of[5], (C,), 0.5, 3.0, ((0, 16),))
    up_weight = scatter_about(key_of[6], (C, HID), C ** -0.5, 0.25, ((0, 16),))
    up_bias = scatter_about(key_of[7], (HID,), 0.5, 3.0, ((0, 16),))
    down_weight = scatter_about(key_of[8], (HID, C), HID ** -0.5, 0.125, ((0, 16),))
    down_bias = scatter_about(key_of[9], (C,), 0.5, 3.0, ((0, 16),))
    return dict(features=features, cotangent=cotangent, depth_weight=depth_weight, depth_bias=depth_bias, norm_gain=norm_gain, norm_shift=norm_shift, up_weight=up_weight, up_bias=up_bias, down_weight=down_weight, down_bias=down_bias)


eps = 1e-06

def gelu_value(value):
    return 0.5 * value * (1.0 + lax.erf(value * (1.0 / math.sqrt(2.0))))

def gelu_slope(value):
    cumulative = 0.5 * (1.0 + lax.erf(value * (1.0 / math.sqrt(2.0))))
    density = jnp.exp(-0.5 * value * value) * (1.0 / math.sqrt(2.0 * math.pi))
    return cumulative + value * density

def depth_conv(padded, kernel, height, width):
    total = jnp.zeros((height, width, kernel.shape[1]), jnp.float32)
    for first in range(7):
        for second in range(7):
            total = total + padded[first:first + height, second:second + width, :] * kernel[first * 7 + second]
    return total

def depth_conv_back(padded, kernel, height, width):
    total = jnp.zeros((height, width, kernel.shape[1]), jnp.float32)
    for first in range(7):
        for second in range(7):
            total = total + padded[6 - first:6 - first + height, 6 - second:6 - second + width, :] * kernel[first * 7 + second]
    return total

def reference(features, cotangent, depth_weight, depth_bias, norm_gain, norm_shift, up_weight, up_bias, down_weight, down_bias):
    height, width, chans = features.shape
    scale = 1.0 / math.sqrt(TOKENS)
    kernel = depth_weight.astype(jnp.float32)
    padded = jnp.pad(features.astype(jnp.float32), ((3, 3), (3, 3), (0, 0)))
    conv = depth_conv(padded, kernel, height, width) + depth_bias.astype(jnp.float32)
    mean_val = lax.optimization_barrier(jnp.mean(conv, axis=2, keepdims=True))
    centered = conv - mean_val
    var_val = lax.optimization_barrier(jnp.mean(centered * centered, axis=2, keepdims=True))
    inv = lax.rsqrt(var_val + eps)
    normed = centered * inv
    normal_out = (normed * norm_gain.astype(jnp.float32) + norm_shift.astype(jnp.float32)).astype(jnp.bfloat16)
    flat_norm = normal_out.reshape(height * width, chans)
    hidden = jnp.dot(flat_norm, up_weight, preferred_element_type=jnp.float32) + up_bias.astype(jnp.float32)
    act = gelu_value(hidden).astype(jnp.bfloat16)
    mixed = jnp.dot(act, down_weight, preferred_element_type=jnp.float32)
    block_out = (features.astype(jnp.float32) + (mixed + down_bias.astype(jnp.float32)).reshape(height, width, chans)).astype(jnp.bfloat16)
    flat_cot = cotangent.reshape(height * width, chans)
    grad_down_weight = jnp.dot(act.T, flat_cot, preferred_element_type=jnp.float32) * scale
    grad_down_bias = lax.optimization_barrier(jnp.sum(flat_cot.astype(jnp.float32), axis=0)) * scale
    dact = jnp.dot(flat_cot, down_weight.T, preferred_element_type=jnp.float32)
    dhidden = (dact * gelu_slope(hidden)).astype(jnp.bfloat16)
    grad_up_weight = jnp.dot(flat_norm.T, dhidden, preferred_element_type=jnp.float32) * scale
    grad_up_bias = lax.optimization_barrier(jnp.sum(dhidden.astype(jnp.float32), axis=0)) * scale
    dnorm = jnp.dot(dhidden, up_weight.T, preferred_element_type=jnp.float32).reshape(height, width, chans)
    grad_norm_gain = lax.optimization_barrier(jnp.sum(dnorm * normed, axis=(0, 1))) * scale
    grad_norm_shift = lax.optimization_barrier(jnp.sum(dnorm, axis=(0, 1))) * scale
    scaled = dnorm * norm_gain.astype(jnp.float32)
    dconv = inv * (scaled - lax.optimization_barrier(jnp.mean(scaled, axis=2, keepdims=True)) - normed * lax.optimization_barrier(jnp.mean(scaled * normed, axis=2, keepdims=True)))
    dconv = dconv.astype(jnp.bfloat16)
    dconv_wide = dconv.astype(jnp.float32)
    back_pad = jnp.pad(dconv_wide, ((3, 3), (3, 3), (0, 0)))
    grad_features = (cotangent.astype(jnp.float32) + depth_conv_back(back_pad, kernel, height, width)).astype(jnp.bfloat16)
    taps = []
    for first in range(7):
        for second in range(7):
            taps.append(lax.optimization_barrier(jnp.sum(dconv_wide * padded[first:first + height, second:second + width, :], axis=(0, 1))))
    grad_depth_weight = jnp.stack(taps, axis=0) * scale
    grad_depth_bias = lax.optimization_barrier(jnp.sum(dconv_wide, axis=(0, 1))) * scale
    return (block_out, grad_features, grad_up_weight, grad_down_weight, grad_depth_weight, grad_depth_bias, grad_norm_gain, grad_norm_shift, grad_up_bias, grad_down_bias)
```

```python
import functools
import math

import jax
import jax.numpy as jnp
from jax import lax
from jax.experimental import pallas as pl
from jax.experimental.pallas import tpu as pltpu
from jax.sharding import PartitionSpec as P

eps = 1e-06
LANES = 128
HALO = 3


class Ring:
    def __init__(self, devices, fold):
        self.devices, self.fold = devices, fold
        self.chips = devices // 2
        self.length = self.chips // fold
        half = self.chips // 2
        rest = self.chips - 1 - half
        self.flows = [(1, 0, half), (-1, 1, half), (-1, 0, rest), (1, 1, rest)]
        self.most = max(half, 1)

    def place(self, chip):
        major, minor = chip // self.fold, chip % self.fold
        return minor * (2 * self.length - 1) + major * (1 - 2 * minor)

    def chip_at(self, place):
        place = lax.rem(place + 2 * self.chips, self.chips)
        minor = place // self.length
        major = minor * (2 * self.length - 1) + place * (1 - 2 * minor)
        return major * self.fold + minor


def fold_of(mesh):
    line = mesh.devices.reshape(mesh.shape["groups"], mesh.shape["row"])[0]
    spots = [getattr(device, "coords", None) for device in line[::2]]
    if any(spot is None for spot in spots) or len(spots) < 2:
        return 1
    spots = [tuple(spot) for spot in spots]
    varying = [axis for axis in range(3) if len({spot[axis] for spot in spots}) > 1]
    fast = [axis for axis in varying if spots[0][axis] != spots[1][axis]]
    if len(varying) == 2 and len(fast) == 1 and len({spot[fast[0]] for spot in spots}) == 2:
        return 2
    return 1


def greet_all(me, devices):
    barrier = pltpu.get_barrier_semaphore()

    @pl.loop(1, devices)
    def _(step):
        pl.semaphore_signal(barrier, inc=1, device_id={"row": lax.rem(me + step, devices)})

    pl.semaphore_wait(barrier, devices - 1)


def send(src, dst, send_sem, recv_sem, target):
    return pltpu.make_async_remote_copy(
        src_ref=src,
        dst_ref=dst,
        send_sem=send_sem,
        recv_sem=recv_sem,
        device_id={"row": target},
        device_id_type=pl.DeviceIdType.MESH,
    )


def gather_kernel(
    ring, up, down, small, feat,
    all_up, all_down, all_small, rim,
    ring_out, ring_in, pair_out, pair_in, small_out, small_in, rim_out, rim_in, own_sem,
):
    devices = ring.devices
    me = lax.axis_index("row")
    core, chip = me % 2, me // 2
    partner = me + 1 - 2 * core
    place = ring.place(chip)
    mine, gathered = (up, down), (all_up, all_down)
    greet_all(me, devices)
    height = feat.shape[0]

    def lower_rim():
        return send(feat.at[pl.ds(height - HALO, HALO)], rim.at[0], rim_out.at[0], rim_in.at[0], lax.rem(me + 1, devices))

    def upper_rim():
        return send(feat.at[pl.ds(0, HALO)], rim.at[1], rim_out.at[1], rim_in.at[1], lax.rem(me + devices - 1, devices))

    @pl.when(me < devices - 1)
    def _():
        lower_rim().start()

    @pl.when(me > 0)
    def _():
        upper_rim().start()

    def small_copy(step):
        return send(small, all_small.at[me], small_out.at[step], small_in.at[step], lax.rem(me + step, devices))

    def small_arrival(step):
        source = lax.rem(me + devices - step, devices)
        return send(small, all_small.at[source], small_out.at[step], small_in.at[step], source)

    @pl.loop(1, devices)
    def _(step):
        small_copy(step).start()

    def owner(flow, step):
        return ring.chip_at(place - ring.flows[flow][0] * step) * 2 + core

    def hop(flow, step):
        direction, which, _ = ring.flows[flow]
        slot = owner(flow, step - 1)
        src = mine[which] if step == 1 else gathered[which].at[slot]
        target = ring.chip_at(place + direction) * 2 + core
        return send(src, gathered[which].at[slot], ring_out.at[flow, step - 1], ring_in.at[flow, step - 1], target)

    def hop_arrival(flow, step):
        direction, which, _ = ring.flows[flow]
        slot = owner(flow, step)
        source = ring.chip_at(place - direction) * 2 + core
        ref = gathered[which].at[slot]
        return send(ref, ref, ring_out.at[flow, step - 1], ring_in.at[flow, step - 1], source)

    def hand(flow, step):
        which = ring.flows[flow][1]
        slot = me if step == 0 else owner(flow, step)
        src = mine[which] if step == 0 else gathered[which].at[slot]
        return send(src, gathered[which].at[slot], pair_out.at[flow, step], pair_in.at[flow, step], partner)

    def hand_arrival(flow, step):
        which = ring.flows[flow][1]
        slot = (partner if step == 0 else ring.chip_at(place - ring.flows[flow][0] * step) * 2 + 1 - core)
        ref = gathered[which].at[slot]
        return send(ref, ref, pair_out.at[flow, step], pair_in.at[flow, step], partner)

    flows = range(len(ring.flows))
    for step in range(1, ring.most + 1):
        for flow in flows:
            hops = ring.flows[flow][2]
            if step <= hops:
                if step > 1:
                    hop_arrival(flow, step - 1).wait_recv()
                hop(flow, step).start()
                if step > 1:
                    hand(flow, step - 1).start()
        if step == 1:
            for flow in (0, 1):
                hand(flow, 0).start()
            owns = [
                pltpu.make_async_copy(up, all_up.at[me], own_sem.at[0]),
                pltpu.make_async_copy(down, all_down.at[me], own_sem.at[1]),
                pltpu.make_async_copy(small, all_small.at[me], own_sem.at[2]),
            ]
            for own in owns:
                own.start()

            @pl.when(me == 0)
            def _():
                rim[0] = jnp.zeros(rim.shape[1:], rim.dtype)

            @pl.when(me == devices - 1)
            def _():
                rim[1] = jnp.zeros(rim.shape[1:], rim.dtype)

    for flow in flows:
        hops = ring.flows[flow][2]
        hop_arrival(flow, hops).wait_recv()
        hand(flow, hops).start()
    for flow in flows:
        hops = ring.flows[flow][2]
        for step in range(0 if flow < 2 else 1, hops + 1):
            hand_arrival(flow, step).wait_recv()
            hand(flow, step).wait_send()
        for step in range(1, hops + 1):
            hop(flow, step).wait_send()

    @pl.loop(1, devices)
    def _(step):
        small_arrival(step).wait_recv()
        small_copy(step).wait_send()

    for own in owns:
        own.wait()

    @pl.when(me < devices - 1)
    def _():
        lower_rim().wait_send()
        upper_rim().wait_recv()

    @pl.when(me > 0)
    def _():
        upper_rim().wait_send()
        lower_rim().wait_recv()


def scatter_kernel(
    ring, up, down, small,
    own_up, own_down, own_small,
    half_up, half_down, got_up, got_down, out_up, out_down, got_small,
    ring_out, ring_in, pair_out, pair_in, small_out, small_in,
):
    devices = ring.devices
    me = lax.axis_index("row")
    core, chip = me % 2, me // 2
    partner = me + 1 - 2 * core
    place = ring.place(chip)
    parts, halves = (up, down), (half_up, half_down)
    got, out, total = (got_up, got_down), (out_up, out_down), (own_up, own_down)
    greet_all(me, devices)

    def pair(which, offset):
        slot = ring.chip_at(place + offset)
        return send(
            parts[which].at[slot, 1 - core], halves[which].at[offset],
            pair_out.at[which, offset], pair_in.at[which, offset], partner,
        )

    half = ring.chips // 2
    order = [half]
    for near in range(half - 1, 0, -1):
        order += [near, ring.chips - near]
    order.append(0)
    for offset in order:
        for which in (0, 1):
            pair(which, offset).start()

    def small_copy(step):
        target = lax.rem(me + step, devices)
        return send(small.at[target], got_small.at[step], small_out.at[step], small_in.at[step], target)

    @pl.loop(1, devices)
    def _(step):
        small_copy(step).start()

    def hop(flow, step):
        direction, which, _ = ring.flows[flow]
        side = 0 if direction > 0 else 1
        target = ring.chip_at(place + direction) * 2 + core
        return send(
            out[which].at[side, step - 1], got[which].at[side, step - 1],
            ring_out.at[flow, step - 1], ring_in.at[flow, step - 1], target,
        )

    known = set()

    def chip_sum(which, offset):
        offset = offset % ring.chips
        if (which, offset) not in known:
            pair(which, offset).wait_recv()
            known.add((which, offset))
        slot = ring.chip_at(place + offset)
        return parts[which][slot, core].astype(jnp.float32) + halves[which][offset].astype(jnp.float32)

    flows = range(len(ring.flows))
    for step in range(1, ring.most + 1):
        for flow in flows:
            direction, which, hops = ring.flows[flow]
            side = 0 if direction > 0 else 1
            if step <= hops:
                value = chip_sum(which, direction * (hops - step + 1))
                if step > 1:
                    hop(flow, step - 1).wait_recv()
                    value = value + got[which][side, step - 2].astype(jnp.float32)
                out[which][side, step - 1] = value.astype(out[which].dtype)
                hop(flow, step).start()

    step_sum = small[me]
    for step in range(1, devices):
        small_copy(step).wait_recv()
        step_sum = step_sum + got_small[step]
    own_small[...] = step_sum
    for which in (0, 1):
        value = chip_sum(which, 0)
        for flow in flows:
            direction, flow_which, hops = ring.flows[flow]
            side = 0 if direction > 0 else 1
            if flow_which == which:
                hop(flow, hops).wait_recv()
                value = value + got[which][side, hops - 1].astype(jnp.float32)
        total[which][...] = value

    for offset in order:
        for which in (0, 1):
            pair(which, offset).wait_send()
    for flow in flows:
        for step in range(1, ring.flows[flow][2] + 1):
            hop(flow, step).wait_send()

    @pl.loop(1, devices)
    def _(step):
        small_copy(step).wait_send()


def vmem():
    return pl.BlockSpec(memory_space=pltpu.VMEM)


def gather(ring, up, down, small, feat):
    devices, most, flows = ring.devices, ring.most, len(ring.flows)
    dma = pltpu.SemaphoreType.DMA
    return pl.pallas_call(
        functools.partial(gather_kernel, ring),
        out_shape=(
            jax.ShapeDtypeStruct((devices,) + up.shape, up.dtype),
            jax.ShapeDtypeStruct((devices,) + down.shape, down.dtype),
            jax.ShapeDtypeStruct((devices,) + small.shape, small.dtype),
            jax.ShapeDtypeStruct((2, HALO) + feat.shape[1:], feat.dtype),
        ),
        in_specs=[vmem()] * 4,
        out_specs=(vmem(),) * 4,
        scratch_shapes=[
            dma((flows, most)), dma((flows, most)),
            dma((flows, most + 1)), dma((flows, most + 1)),
            dma((devices,)), dma((devices,)),
            dma((2,)), dma((2,)), dma((3,)),
        ],
        compiler_params=pltpu.CompilerParams(
            collective_id=0, has_side_effects=True, vmem_limit_bytes=56 * 2**20
        ),
        name="gather",
    )(up, down, small, feat)


def scatter(ring, up, down, small):
    devices, most, flows, chips = ring.devices, ring.most, len(ring.flows), ring.chips
    dma = pltpu.SemaphoreType.DMA
    block_up, block_down = up.shape[2:], down.shape[2:]
    kind = up.dtype
    return pl.pallas_call(
        functools.partial(scatter_kernel, ring),
        out_shape=(
            jax.ShapeDtypeStruct(block_up, jnp.float32),
            jax.ShapeDtypeStruct(block_down, jnp.float32),
            jax.ShapeDtypeStruct(small.shape[1:], jnp.float32),
        ),
        in_specs=[vmem()] * 3,
        out_specs=(vmem(),) * 3,
        scratch_shapes=[
            pltpu.VMEM((chips,) + block_up, kind),
            pltpu.VMEM((chips,) + block_down, kind),
            pltpu.VMEM((2, most) + block_up, kind),
            pltpu.VMEM((2, most) + block_down, kind),
            pltpu.VMEM((2, most) + block_up, kind),
            pltpu.VMEM((2, most) + block_down, kind),
            pltpu.VMEM(small.shape, jnp.float32),
            dma((flows, most)), dma((flows, most)),
            dma((2, chips)), dma((2, chips)),
            dma((devices,)), dma((devices,)),
        ],
        compiler_params=pltpu.CompilerParams(
            collective_id=1, has_side_effects=True, vmem_limit_bytes=56 * 2**20
        ),
        name="scatter",
    )(up, down, small)


def gelu_parts(value):
    cumulative = 0.5 * (1.0 + lax.erf(value * (1.0 / math.sqrt(2.0))))
    density = jnp.exp(-0.5 * value * value) * (1.0 / math.sqrt(2.0 * math.pi))
    return value * cumulative, cumulative + value * density


def depth_conv(padded, kernel, height, width, flip):
    total = jnp.zeros((height, width, kernel.shape[1]), jnp.float32)
    for first in range(7):
        for second in range(7):
            top, left = (6 - first, 6 - second) if flip else (first, second)
            total = total + padded[top : top + height, left : left + width, :] * kernel[first * 7 + second]
    return total


def per_device(
    ring,
    features,
    cotangent,
    depth_weight,
    depth_bias,
    norm_gain,
    norm_shift,
    up_weight,
    up_bias,
    down_weight,
    down_bias,
):
    height, width, chans = features.shape
    devices = ring.devices
    cells = height * width
    own = chans // devices
    units = up_weight.shape[1]
    ratio = units // chans
    scale = 1.0 / math.sqrt(cells * devices)
    packed = jnp.concatenate(
        [depth_weight, depth_bias[None], norm_gain[None], norm_shift[None], down_bias[None], up_bias.reshape(ratio, own)],
        axis=0,
    )
    rows = packed.shape[0]
    filled = -(-rows // 64) * 64
    packed = jnp.pad(packed, ((0, filled - rows), (0, 0))).reshape(filled * own // LANES, LANES)
    all_up, all_down, all_small, rim = gather(ring, up_weight, down_weight, packed, features)
    up_full = all_up.reshape(chans, units)
    down_full = all_down.reshape(units, chans)
    all_small = all_small.reshape(devices, filled, own).transpose(1, 0, 2)
    wide = all_small.reshape(filled, chans).astype(jnp.float32)
    taps = depth_weight.shape[0]
    kernel, conv_bias, gain, shift, bias_down = wide[:taps], wide[taps], wide[taps + 1], wide[taps + 2], wide[taps + 3]
    bias_up = all_small[taps + 4 : taps + 4 + ratio].transpose(1, 0, 2).reshape(units).astype(jnp.float32)

    rimmed = jnp.concatenate([rim[0], features, rim[1]], axis=0)
    padded = jnp.pad(rimmed.astype(jnp.float32), ((0, 0), (3, 3), (0, 0)))
    conv = depth_conv(padded, kernel, height, width, False) + conv_bias
    mean_val = jnp.mean(conv, axis=2, keepdims=True)
    centered = conv - mean_val
    var_val = jnp.mean(centered * centered, axis=2, keepdims=True)
    inv = lax.rsqrt(var_val + eps)
    normed = centered * inv
    flat_norm = (normed * gain + shift).astype(jnp.bfloat16).reshape(cells, chans)
    flat_cot = cotangent.reshape(cells, chans)
    hidden = jnp.dot(flat_norm, up_full, preferred_element_type=jnp.float32) + bias_up
    act, slope = gelu_parts(hidden)
    act = act.astype(jnp.bfloat16)
    mixed = jnp.dot(act, down_full, preferred_element_type=jnp.float32)
    block_out = (features.astype(jnp.float32) + (mixed + bias_down).reshape(height, width, chans)).astype(jnp.bfloat16)
    kind = jnp.bfloat16
    down_part = (
        lax.dot_general(act, flat_cot, (((0,), (0,)), ((), ())), preferred_element_type=jnp.float32) * scale
    ).astype(kind)
    dact = lax.dot_general(flat_cot, down_full, (((1,), (1,)), ((), ())), preferred_element_type=jnp.float32)
    dhidden = (dact * slope).astype(jnp.bfloat16)
    up_part = (
        lax.dot_general(flat_norm, dhidden, (((0,), (0,)), ((), ())), preferred_element_type=jnp.float32) * scale
    ).astype(kind)
    dnorm = lax.dot_general(dhidden, up_full, (((1,), (1,)), ((), ())), preferred_element_type=jnp.float32)
    dnorm = dnorm.reshape(height, width, chans)
    down_bias_term = jnp.sum(flat_cot.astype(jnp.float32), axis=0)
    up_bias_term = jnp.sum(dhidden.astype(jnp.float32), axis=0)
    gain_term = jnp.sum(dnorm * normed, axis=(0, 1))
    shift_term = jnp.sum(dnorm, axis=(0, 1))
    scaled = dnorm * gain
    dconv = inv * (
        scaled
        - jnp.mean(scaled, axis=2, keepdims=True)
        - normed * jnp.mean(scaled * normed, axis=2, keepdims=True)
    )
    dconv = dconv.astype(jnp.bfloat16)
    forward = [(i, i + 1) for i in range(devices - 1)]
    backward = [(i + 1, i) for i in range(devices - 1)]
    low = lax.ppermute(dconv[height - HALO :], "row", forward)
    high = lax.ppermute(dconv[:HALO], "row", backward)
    dconv_wide = dconv.astype(jnp.float32)
    tap_terms = []
    for first in range(7):
        for second in range(7):
            tap_terms.append(
                jnp.sum(dconv_wide * padded[first : first + height, second : second + width, :], axis=(0, 1))
            )
    conv_bias_term = jnp.sum(dconv_wide, axis=(0, 1))
    terms = jnp.concatenate(
        [
            jnp.stack(tap_terms + [conv_bias_term, gain_term, shift_term, down_bias_term], axis=0),
            up_bias_term.reshape(devices, ratio, own).transpose(1, 0, 2).reshape(ratio, chans),
        ],
        axis=0,
    ) * scale
    terms = jnp.pad(terms, ((0, filled - rows), (0, 0)))
    terms = terms.reshape(filled, devices, own).transpose(1, 0, 2).reshape(devices, filled * own // LANES, LANES)
    grad_up, grad_down, own_terms = scatter(
        ring,
        up_part.reshape(ring.chips, 2, chans // devices, units),
        down_part.reshape(ring.chips, 2, units // devices, chans),
        terms,
    )
    own_terms = own_terms.reshape(filled, own)
    back_rim = jnp.concatenate([low, dconv, high], axis=0)
    back_pad = jnp.pad(back_rim.astype(jnp.float32), ((0, 0), (3, 3), (0, 0)))
    grad_features = (
        cotangent.astype(jnp.float32) + depth_conv(back_pad, kernel, height, width, True)
    ).astype(jnp.bfloat16)
    return (
        block_out,
        grad_features,
        grad_up,
        grad_down,
        own_terms[:taps],
        own_terms[taps],
        own_terms[taps + 1],
        own_terms[taps + 2],
        own_terms[taps + 4 : taps + 4 + ratio].reshape(ratio * own),
        own_terms[taps + 3],
    )


def solution(mesh):
    ring = Ring(mesh.shape["row"], fold_of(mesh))
    placed = (
        P(("groups", "row"), None, None),
        P(("groups", "row"), None, None),
        P(None, "row"),
        P("row"),
        P("row"),
        P("row"),
        P("row", None),
        P("row"),
        P("row", None),
        P("row"),
    )
    return jax.shard_map(
        functools.partial(per_device, ring),
        mesh=mesh,
        in_specs=placed,
        out_specs=(
            P(("groups", "row"), None, None),
            P(("groups", "row"), None, None),
            P(("groups", "row"), None),
            P(("groups", "row"), None),
            P("groups", "row"),
            P(("groups", "row")),
            P(("groups", "row")),
            P(("groups", "row")),
            P(("groups", "row")),
            P(("groups", "row")),
        ),
        check_vma=False,
    )
```

```python
import functools
import math

import jax
import jax.numpy as jnp
from jax import lax
from jax.experimental import pallas as pl
from jax.experimental.pallas import tpu as pltpu
from jax.sharding import PartitionSpec as P

eps = 1e-06
LANES = 128
HALO = 3


class Ring:
    def __init__(self, devices, fold):
        self.devices, self.fold = devices, fold
        self.chips = devices // 2
        self.length = self.chips // fold
        half = self.chips // 2
        rest = self.chips - 1 - half
        self.flows = [(1, 0, half), (-1, 1, half), (-1, 0, rest), (1, 1, rest)]
        self.most = max(half, 1)

    def place(self, chip):
        major, minor = chip // self.fold, chip % self.fold
        return minor * (2 * self.length - 1) + major * (1 - 2 * minor)

    def chip_at(self, place):
        place = lax.rem(place + 2 * self.chips, self.chips)
        minor = place // self.length
        major = minor * (2 * self.length - 1) + place * (1 - 2 * minor)
        return major * self.fold + minor


def fold_of(mesh):
    line = mesh.devices.reshape(mesh.shape["groups"], mesh.shape["row"])[0]
    spots = [getattr(device, "coords", None) for device in line[::2]]
    if any(spot is None for spot in spots) or len(spots) < 2:
        return 1
    spots = [tuple(spot) for spot in spots]
    varying = [axis for axis in range(3) if len({spot[axis] for spot in spots}) > 1]
    fast = [axis for axis in varying if spots[0][axis] != spots[1][axis]]
    if len(varying) == 2 and len(fast) == 1 and len({spot[fast[0]] for spot in spots}) == 2:
        return 2
    return 1


def greet_all(me, devices):
    barrier = pltpu.get_barrier_semaphore()

    @pl.loop(1, devices)
    def _(step):
        pl.semaphore_signal(barrier, inc=1, device_id={"row": lax.rem(me + step, devices)})

    pl.semaphore_wait(barrier, devices - 1)


def send(src, dst, send_sem, recv_sem, target):
    return pltpu.make_async_remote_copy(
        src_ref=src,
        dst_ref=dst,
        send_sem=send_sem,
        recv_sem=recv_sem,
        device_id={"row": target},
        device_id_type=pl.DeviceIdType.MESH,
    )


LEFT = 8


def fill_middle(wide_rows, block):
    height, width, _ = block.shape
    wide_rows[...] = jnp.zeros_like(wide_rows)
    for row in range(height):
        wide_rows[HALO + row, LEFT : LEFT + width, :] = block[row].astype(jnp.float32)


def fill_rims(wide_rows, rim, height, width):
    for row in range(HALO):
        wide_rows[row, LEFT : LEFT + width, :] = rim[0, row].astype(jnp.float32)
        wide_rows[HALO + height + row, LEFT : LEFT + width, :] = rim[1, row].astype(jnp.float32)


def conv_row(wide_rows, kernel, row, width, flip, store):
    chans = wide_rows.shape[2]

    @pl.loop(0, chans // LANES)
    def _(group):
        lanes = pl.ds(pl.multiple_of(group * LANES, LANES), LANES)
        total = jnp.zeros((width, LANES), jnp.float32)
        for first in range(7):
            for second in range(7):
                top, left = (6 - first, 6 - second) if flip else (first, second)
                tap = first * 7 + second
                begin = LEFT - HALO + left
                total = total + wide_rows[row + top, begin : begin + width, lanes] * kernel[tap : tap + 1, lanes]
        store(lanes, total)


def unpack(all_small, wide, devices, own):
    pieces = LANES // own
    rows = all_small.shape[1]
    spot = lax.broadcasted_iota(jnp.int32, (rows, LANES), 1) // own
    for group in range(devices // pieces):
        sources = [all_small[group * pieces + part].astype(jnp.float32) for part in range(pieces)]
        for block in range(pieces):
            total = jnp.zeros((rows, LANES), jnp.float32)
            for part in range(pieces):
                shift = ((part - block) * own) % LANES
                moved = sources[part] if shift == 0 else pltpu.roll(sources[part], shift, 1)
                total = jnp.where(spot == part, moved, total)
            wide[block * rows : (block + 1) * rows, group * LANES : (group + 1) * LANES] = total


def rows_at(step, most, height):
    return [row for row in range(height) if min(2, most) + row * (most - 1) // height == step]


def gather_kernel(
    ring, taps, up, down, small, feat,
    all_up, all_down, wide, rim, normed, normal_out, inv_out,
    all_small, wide_rows, conv,
    ring_out, ring_in, pair_out, pair_in, small_out, small_in, rim_out, rim_in, own_sem,
):
    devices = ring.devices
    me = lax.axis_index("row")
    core, chip = me % 2, me // 2
    partner = me + 1 - 2 * core
    place = ring.place(chip)
    mine, gathered = (up, down), (all_up, all_down)
    greet_all(me, devices)
    height, width, chans = feat.shape

    def normalise(row):
        def store(lanes, total):
            conv[:, lanes] = total + wide[taps : taps + 1, lanes]

        conv_row(wide_rows, wide, row, width, False, store)
        value = conv[...]
        centered = value - jnp.mean(value, axis=1, keepdims=True)
        inv = lax.rsqrt(jnp.mean(centered * centered, axis=1, keepdims=True) + eps)
        unit = centered * inv
        normed[row] = unit
        inv_out[row] = inv
        normal_out[row] = (unit * wide[taps + 1 : taps + 2, :] + wide[taps + 2 : taps + 3, :]).astype(normal_out.dtype)

    def lower_rim():
        return send(feat.at[pl.ds(height - HALO, HALO)], rim.at[0], rim_out.at[0], rim_in.at[0], lax.rem(me + 1, devices))

    def upper_rim():
        return send(feat.at[pl.ds(0, HALO)], rim.at[1], rim_out.at[1], rim_in.at[1], lax.rem(me + devices - 1, devices))

    @pl.when(me < devices - 1)
    def _():
        lower_rim().start()

    @pl.when(me > 0)
    def _():
        upper_rim().start()

    def small_copy(step):
        return send(small, all_small.at[me], small_out.at[step], small_in.at[step], lax.rem(me + step, devices))

    def small_arrival(step):
        source = lax.rem(me + devices - step, devices)
        return send(small, all_small.at[source], small_out.at[step], small_in.at[step], source)

    @pl.loop(1, devices)
    def _(step):
        small_copy(step).start()

    def owner(flow, step):
        return ring.chip_at(place - ring.flows[flow][0] * step) * 2 + core

    def hop(flow, step):
        direction, which, _ = ring.flows[flow]
        slot = owner(flow, step - 1)
        src = mine[which] if step == 1 else gathered[which].at[slot]
        target = ring.chip_at(place + direction) * 2 + core
        return send(src, gathered[which].at[slot], ring_out.at[flow, step - 1], ring_in.at[flow, step - 1], target)

    def hop_arrival(flow, step):
        direction, which, _ = ring.flows[flow]
        slot = owner(flow, step)
        source = ring.chip_at(place - direction) * 2 + core
        ref = gathered[which].at[slot]
        return send(ref, ref, ring_out.at[flow, step - 1], ring_in.at[flow, step - 1], source)

    def hand(flow, step):
        which = ring.flows[flow][1]
        slot = me if step == 0 else owner(flow, step)
        src = mine[which] if step == 0 else gathered[which].at[slot]
        return send(src, gathered[which].at[slot], pair_out.at[flow, step], pair_in.at[flow, step], partner)

    def hand_arrival(flow, step):
        which = ring.flows[flow][1]
        slot = (partner if step == 0 else ring.chip_at(place - ring.flows[flow][0] * step) * 2 + 1 - core)
        ref = gathered[which].at[slot]
        return send(ref, ref, pair_out.at[flow, step], pair_in.at[flow, step], partner)

    flows = range(len(ring.flows))
    for step in range(1, ring.most + 1):
        for flow in flows:
            hops = ring.flows[flow][2]
            if step <= hops:
                if step > 1:
                    hop_arrival(flow, step - 1).wait_recv()
                hop(flow, step).start()
                if step > 1:
                    hand(flow, step - 1).start()
        if step == 1:
            for flow in (0, 1):
                hand(flow, 0).start()
            fill_middle(wide_rows, feat)
            owns = [
                pltpu.make_async_copy(up, all_up.at[me], own_sem.at[0]),
                pltpu.make_async_copy(down, all_down.at[me], own_sem.at[1]),
                pltpu.make_async_copy(small, all_small.at[me], own_sem.at[2]),
            ]
            for own in owns:
                own.start()

            @pl.when(me == 0)
            def _():
                rim[0] = jnp.zeros(rim.shape[1:], rim.dtype)

            @pl.when(me == devices - 1)
            def _():
                rim[1] = jnp.zeros(rim.shape[1:], rim.dtype)

            owns[2].wait()

            @pl.loop(1, devices)
            def _(other):
                small_arrival(other).wait_recv()

            unpack(all_small, wide, devices, chans // devices)

            @pl.when(me < devices - 1)
            def _():
                upper_rim().wait_recv()

            @pl.when(me > 0)
            def _():
                lower_rim().wait_recv()

            fill_rims(wide_rows, rim, height, width)
        for row in rows_at(step, ring.most, height):
            normalise(row)

    for flow in flows:
        hops = ring.flows[flow][2]
        hop_arrival(flow, hops).wait_recv()
        hand(flow, hops).start()
    for flow in flows:
        hops = ring.flows[flow][2]
        for step in range(0 if flow < 2 else 1, hops + 1):
            hand_arrival(flow, step).wait_recv()
            hand(flow, step).wait_send()
        for step in range(1, hops + 1):
            hop(flow, step).wait_send()

    @pl.loop(1, devices)
    def _(step):
        small_copy(step).wait_send()

    for own in owns[:2]:
        own.wait()

    @pl.when(me < devices - 1)
    def _():
        lower_rim().wait_send()

    @pl.when(me > 0)
    def _():
        upper_rim().wait_send()


def scatter_kernel(
    ring, up, down, small, dconv, wide, cot,
    own_up, own_down, own_small, grad_feat,
    half_up, half_down, got_up, got_down, out_up, out_down, got_small, rim, wide_rows,
    ring_out, ring_in, pair_out, pair_in, small_out, small_in, rim_out, rim_in,
):
    devices = ring.devices
    me = lax.axis_index("row")
    core, chip = me % 2, me // 2
    partner = me + 1 - 2 * core
    place = ring.place(chip)
    parts, halves = (up, down), (half_up, half_down)
    got, out, total = (got_up, got_down), (out_up, out_down), (own_up, own_down)
    greet_all(me, devices)

    height, width, _ = dconv.shape

    def lower_rim():
        return send(dconv.at[pl.ds(height - HALO, HALO)], rim.at[0], rim_out.at[0], rim_in.at[0], lax.rem(me + 1, devices))

    def upper_rim():
        return send(dconv.at[pl.ds(0, HALO)], rim.at[1], rim_out.at[1], rim_in.at[1], lax.rem(me + devices - 1, devices))

    def spread(row):
        def store(lanes, total):
            grad_feat[row, :, lanes] = (cot[row, :, lanes].astype(jnp.float32) + total).astype(grad_feat.dtype)

        conv_row(wide_rows, wide, row, width, True, store)

    def pair(which, offset):
        slot = ring.chip_at(place + offset)
        return send(
            parts[which].at[slot, 1 - core], halves[which].at[offset],
            pair_out.at[which, offset], pair_in.at[which, offset], partner,
        )

    half = ring.chips // 2
    order = [half]
    for near in range(half - 1, 0, -1):
        order += [near, ring.chips - near]
    order.append(0)
    for offset in order:
        for which in (0, 1):
            pair(which, offset).start()

    @pl.when(me < devices - 1)
    def _():
        lower_rim().start()

    @pl.when(me > 0)
    def _():
        upper_rim().start()

    def small_copy(step):
        target = lax.rem(me + step, devices)
        return send(small.at[target], got_small.at[step], small_out.at[step], small_in.at[step], target)

    @pl.loop(1, devices)
    def _(step):
        small_copy(step).start()

    def hop(flow, step):
        direction, which, _ = ring.flows[flow]
        side = 0 if direction > 0 else 1
        target = ring.chip_at(place + direction) * 2 + core
        return send(
            out[which].at[side, step - 1], got[which].at[side, step - 1],
            ring_out.at[flow, step - 1], ring_in.at[flow, step - 1], target,
        )

    known = set()

    def chip_sum(which, offset):
        offset = offset % ring.chips
        if (which, offset) not in known:
            pair(which, offset).wait_recv()
            known.add((which, offset))
        slot = ring.chip_at(place + offset)
        return parts[which][slot, core].astype(jnp.float32) + halves[which][offset].astype(jnp.float32)

    flows = range(len(ring.flows))
    for step in range(1, ring.most + 1):
        for flow in flows:
            direction, which, hops = ring.flows[flow]
            side = 0 if direction > 0 else 1
            if step <= hops:
                value = chip_sum(which, direction * (hops - step + 1))
                if step > 1:
                    hop(flow, step - 1).wait_recv()
                    value = value + got[which][side, step - 2].astype(jnp.float32)
                out[which][side, step - 1] = value.astype(out[which].dtype)
                hop(flow, step).start()
        if step == 1:
            fill_middle(wide_rows, dconv)

            @pl.when(me == 0)
            def _():
                rim[0] = jnp.zeros(rim.shape[1:], rim.dtype)

            @pl.when(me == devices - 1)
            def _():
                rim[1] = jnp.zeros(rim.shape[1:], rim.dtype)

            @pl.when(me < devices - 1)
            def _():
                upper_rim().wait_recv()

            @pl.when(me > 0)
            def _():
                lower_rim().wait_recv()

            fill_rims(wide_rows, rim, height, width)
        for row in rows_at(step, ring.most, height):
            spread(row)

    step_sum = small[me]
    for step in range(1, devices):
        small_copy(step).wait_recv()
        step_sum = step_sum + got_small[step]
    own_small[...] = step_sum
    for which in (0, 1):
        value = chip_sum(which, 0)
        for flow in flows:
            direction, flow_which, hops = ring.flows[flow]
            side = 0 if direction > 0 else 1
            if flow_which == which:
                hop(flow, hops).wait_recv()
                value = value + got[which][side, hops - 1].astype(jnp.float32)
        total[which][...] = value

    for offset in order:
        for which in (0, 1):
            pair(which, offset).wait_send()
    for flow in flows:
        for step in range(1, ring.flows[flow][2] + 1):
            hop(flow, step).wait_send()

    @pl.loop(1, devices)
    def _(step):
        small_copy(step).wait_send()

    @pl.when(me < devices - 1)
    def _():
        lower_rim().wait_send()

    @pl.when(me > 0)
    def _():
        upper_rim().wait_send()


def vmem():
    return pl.BlockSpec(memory_space=pltpu.VMEM)


def gather(ring, taps, filled, up, down, small, feat):
    height, width, chans = feat.shape
    devices, most, flows = ring.devices, ring.most, len(ring.flows)
    dma = pltpu.SemaphoreType.DMA
    return pl.pallas_call(
        functools.partial(gather_kernel, ring, taps),
        out_shape=(
            jax.ShapeDtypeStruct((devices,) + up.shape, up.dtype),
            jax.ShapeDtypeStruct((devices,) + down.shape, down.dtype),
            jax.ShapeDtypeStruct((filled, chans), jnp.float32),
            jax.ShapeDtypeStruct((2, HALO) + feat.shape[1:], feat.dtype),
            jax.ShapeDtypeStruct(feat.shape, jnp.float32),
            jax.ShapeDtypeStruct(feat.shape, jnp.bfloat16),
            jax.ShapeDtypeStruct((height, width, 1), jnp.float32),
        ),
        in_specs=[vmem()] * 4,
        out_specs=(vmem(),) * 7,
        scratch_shapes=[
            pltpu.VMEM((devices,) + small.shape, small.dtype),
            pltpu.VMEM((height + 2 * HALO, width + 2 * LEFT, chans), jnp.float32),
            pltpu.VMEM((width, chans), jnp.float32),
            dma((flows, most)), dma((flows, most)),
            dma((flows, most + 1)), dma((flows, most + 1)),
            dma((devices,)), dma((devices,)),
            dma((2,)), dma((2,)), dma((3,)),
        ],
        compiler_params=pltpu.CompilerParams(
            collective_id=0, has_side_effects=True, vmem_limit_bytes=56 * 2**20
        ),
        name="gather",
    )(up, down, small, feat)


def scatter(ring, up, down, small, dconv, wide, cot):
    height, width, chans = dconv.shape
    devices, most, flows, chips = ring.devices, ring.most, len(ring.flows), ring.chips
    dma = pltpu.SemaphoreType.DMA
    block_up, block_down = up.shape[2:], down.shape[2:]
    kind = up.dtype
    return pl.pallas_call(
        functools.partial(scatter_kernel, ring),
        out_shape=(
            jax.ShapeDtypeStruct(block_up, jnp.float32),
            jax.ShapeDtypeStruct(block_down, jnp.float32),
            jax.ShapeDtypeStruct(small.shape[1:], jnp.float32),
            jax.ShapeDtypeStruct(cot.shape, cot.dtype),
        ),
        in_specs=[vmem()] * 6,
        out_specs=(vmem(),) * 4,
        scratch_shapes=[
            pltpu.VMEM((chips,) + block_up, kind),
            pltpu.VMEM((chips,) + block_down, kind),
            pltpu.VMEM((2, most) + block_up, kind),
            pltpu.VMEM((2, most) + block_down, kind),
            pltpu.VMEM((2, most) + block_up, kind),
            pltpu.VMEM((2, most) + block_down, kind),
            pltpu.VMEM(small.shape, jnp.float32),
            pltpu.VMEM((2, HALO, width, chans), dconv.dtype),
            pltpu.VMEM((height + 2 * HALO, width + 2 * LEFT, chans), jnp.float32),
            dma((flows, most)), dma((flows, most)),
            dma((2, chips)), dma((2, chips)),
            dma((devices,)), dma((devices,)),
            dma((2,)), dma((2,)),
        ],
        compiler_params=pltpu.CompilerParams(
            collective_id=1, has_side_effects=True, vmem_limit_bytes=56 * 2**20
        ),
        name="scatter",
    )(up, down, small, dconv, wide, cot)


def gelu_parts(value):
    cumulative = 0.5 * (1.0 + lax.erf(value * (1.0 / math.sqrt(2.0))))
    density = jnp.exp(-0.5 * value * value) * (1.0 / math.sqrt(2.0 * math.pi))
    return value * cumulative, cumulative + value * density


def per_device(
    ring,
    features,
    cotangent,
    depth_weight,
    depth_bias,
    norm_gain,
    norm_shift,
    up_weight,
    up_bias,
    down_weight,
    down_bias,
):
    height, width, chans = features.shape
    devices = ring.devices
    cells = height * width
    own = chans // devices
    units = up_weight.shape[1]
    ratio = units // chans
    scale = 1.0 / math.sqrt(cells * devices)
    packed = jnp.concatenate(
        [depth_weight, depth_bias[None], norm_gain[None], norm_shift[None], down_bias[None], up_bias.reshape(ratio, own)],
        axis=0,
    )
    rows = packed.shape[0]
    filled = -(-rows // 64) * 64
    pieces = LANES // own
    packed = jnp.pad(packed, ((0, filled - rows), (0, 0)))
    packed = packed.reshape(pieces, filled // pieces, own).transpose(1, 0, 2).reshape(filled // pieces, LANES)
    taps = depth_weight.shape[0]
    all_up, all_down, wide, rim, normed, normal_out, inv = gather(
        ring, taps, filled, up_weight, down_weight, packed, features
    )
    up_full = all_up.reshape(chans, units)
    down_full = all_down.reshape(units, chans)
    gain, bias_down = wide[taps + 1], wide[taps + 3]
    bias_up = wide[taps + 4 : taps + 4 + ratio].reshape(ratio, devices, own).transpose(1, 0, 2).reshape(units)
    rimmed = jnp.concatenate([rim[0], features, rim[1]], axis=0)
    padded = jnp.pad(rimmed.astype(jnp.float32), ((0, 0), (3, 3), (0, 0)))
    flat_norm = normal_out.reshape(cells, chans)
    flat_cot = cotangent.reshape(cells, chans)
    hidden = jnp.dot(flat_norm, up_full, preferred_element_type=jnp.float32) + bias_up
    act, slope = gelu_parts(hidden)
    act = act.astype(jnp.bfloat16)
    mixed = jnp.dot(act, down_full, preferred_element_type=jnp.float32)
    block_out = (features.astype(jnp.float32) + (mixed + bias_down).reshape(height, width, chans)).astype(jnp.bfloat16)
    kind = jnp.bfloat16
    down_part = (
        lax.dot_general(act, flat_cot, (((0,), (0,)), ((), ())), preferred_element_type=jnp.float32) * scale
    ).astype(kind)
    dact = lax.dot_general(flat_cot, down_full, (((1,), (1,)), ((), ())), preferred_element_type=jnp.float32)
    dhidden = (dact * slope).astype(jnp.bfloat16)
    up_part = (
        lax.dot_general(flat_norm, dhidden, (((0,), (0,)), ((), ())), preferred_element_type=jnp.float32) * scale
    ).astype(kind)
    dnorm = lax.dot_general(dhidden, up_full, (((1,), (1,)), ((), ())), preferred_element_type=jnp.float32)
    dnorm = dnorm.reshape(height, width, chans)
    down_bias_term = jnp.sum(flat_cot.astype(jnp.float32), axis=0)
    up_bias_term = jnp.sum(dhidden.astype(jnp.float32), axis=0)
    gain_term = jnp.sum(dnorm * normed, axis=(0, 1))
    shift_term = jnp.sum(dnorm, axis=(0, 1))
    scaled = dnorm * gain
    dconv = inv * (
        scaled
        - jnp.mean(scaled, axis=2, keepdims=True)
        - normed * jnp.mean(scaled * normed, axis=2, keepdims=True)
    )
    dconv = dconv.astype(jnp.bfloat16)
    dconv_wide = dconv.astype(jnp.float32)
    tap_terms = []
    for first in range(7):
        for second in range(7):
            tap_terms.append(
                jnp.sum(dconv_wide * padded[first : first + height, second : second + width, :], axis=(0, 1))
            )
    conv_bias_term = jnp.sum(dconv_wide, axis=(0, 1))
    terms = jnp.concatenate(
        [
            jnp.stack(tap_terms + [conv_bias_term, gain_term, shift_term, down_bias_term], axis=0),
            up_bias_term.reshape(devices, ratio, own).transpose(1, 0, 2).reshape(ratio, chans),
        ],
        axis=0,
    ) * scale
    terms = jnp.pad(terms, ((0, filled - rows), (0, 0)))
    terms = terms.reshape(filled, devices, own).transpose(1, 0, 2).reshape(devices, filled * own // LANES, LANES)
    grad_up, grad_down, own_terms, grad_features = scatter(
        ring,
        up_part.reshape(ring.chips, 2, chans // devices, units),
        down_part.reshape(ring.chips, 2, units // devices, chans),
        terms,
        dconv,
        wide,
        cotangent,
    )
    own_terms = own_terms.reshape(filled, own)
    return (
        block_out,
        grad_features,
        grad_up,
        grad_down,
        own_terms[:taps],
        own_terms[taps],
        own_terms[taps + 1],
        own_terms[taps + 2],
        own_terms[taps + 4 : taps + 4 + ratio].reshape(ratio * own),
        own_terms[taps + 3],
    )


def solution(mesh):
    ring = Ring(mesh.shape["row"], fold_of(mesh))
    placed = (
        P(("groups", "row"), None, None),
        P(("groups", "row"), None, None),
        P(None, "row"),
        P("row"),
        P("row"),
        P("row"),
        P("row", None),
        P("row"),
        P("row", None),
        P("row"),
    )
    return jax.shard_map(
        functools.partial(per_device, ring),
        mesh=mesh,
        in_specs=placed,
        out_specs=(
            P(("groups", "row"), None, None),
            P(("groups", "row"), None, None),
            P(("groups", "row"), None),
            P(("groups", "row"), None),
            P("groups", "row"),
            P(("groups", "row")),
            P(("groups", "row")),
            P(("groups", "row")),
            P(("groups", "row")),
            P(("groups", "row")),
        ),
        check_vma=False,
    )
```

```python
import functools
import math

import jax
import jax.numpy as jnp
from jax import lax
from jax.experimental import pallas as pl
from jax.experimental.pallas import tpu as pltpu
from jax.sharding import PartitionSpec as P

eps = 1e-06
LANES = 128
HALO = 3


class Ring:
    def __init__(self, devices, fold):
        self.devices, self.fold = devices, fold
        self.chips = devices // 2
        self.length = self.chips // fold
        half = self.chips // 2
        rest = self.chips - 1 - half
        self.flows = [(1, 0, half), (-1, 1, half), (-1, 0, rest), (1, 1, rest)]
        self.most = max(half, 1)

    def place(self, chip):
        major, minor = chip // self.fold, chip % self.fold
        return minor * (2 * self.length - 1) + major * (1 - 2 * minor)

    def chip_at(self, place):
        place = lax.rem(place + 2 * self.chips, self.chips)
        minor = place // self.length
        major = minor * (2 * self.length - 1) + place * (1 - 2 * minor)
        return major * self.fold + minor


def fold_of(mesh):
    line = mesh.devices.reshape(mesh.shape["groups"], mesh.shape["row"])[0]
    spots = [getattr(device, "coords", None) for device in line[::2]]
    if any(spot is None for spot in spots) or len(spots) < 2:
        return 1
    spots = [tuple(spot) for spot in spots]
    varying = [axis for axis in range(3) if len({spot[axis] for spot in spots}) > 1]
    fast = [axis for axis in varying if spots[0][axis] != spots[1][axis]]
    if len(varying) == 2 and len(fast) == 1 and len({spot[fast[0]] for spot in spots}) == 2:
        return 2
    return 1


def greet_all(me, devices):
    barrier = pltpu.get_barrier_semaphore()

    @pl.loop(1, devices)
    def _(step):
        pl.semaphore_signal(barrier, inc=1, device_id={"row": lax.rem(me + step, devices)})

    pl.semaphore_wait(barrier, devices - 1)


def send(src, dst, send_sem, recv_sem, target):
    return pltpu.make_async_remote_copy(
        src_ref=src,
        dst_ref=dst,
        send_sem=send_sem,
        recv_sem=recv_sem,
        device_id={"row": target},
        device_id_type=pl.DeviceIdType.MESH,
    )


LEFT = 8


def fill_middle(wide_rows, block):
    height, width, _ = block.shape
    wide_rows[...] = jnp.zeros_like(wide_rows)
    for row in range(height):
        wide_rows[HALO + row, LEFT : LEFT + width, :] = block[row].astype(jnp.float32)


def fill_rims(wide_rows, rim, height, width):
    for row in range(HALO):
        wide_rows[row, LEFT : LEFT + width, :] = rim[0, row].astype(jnp.float32)
        wide_rows[HALO + height + row, LEFT : LEFT + width, :] = rim[1, row].astype(jnp.float32)


def conv_row(wide_rows, kernel, row, width, flip, store):
    chans = wide_rows.shape[2]

    @pl.loop(0, chans // LANES)
    def _(group):
        lanes = pl.ds(pl.multiple_of(group * LANES, LANES), LANES)
        total = jnp.zeros((width, LANES), jnp.float32)
        for first in range(7):
            for second in range(7):
                top, left = (6 - first, 6 - second) if flip else (first, second)
                tap = first * 7 + second
                begin = LEFT - HALO + left
                total = total + wide_rows[row + top, begin : begin + width, lanes] * kernel[tap : tap + 1, lanes]
        store(lanes, total)


def unpack(all_small, wide, devices, own):
    pieces = LANES // own
    rows = all_small.shape[1]
    spot = lax.broadcasted_iota(jnp.int32, (rows, LANES), 1) // own
    for group in range(devices // pieces):
        sources = [all_small[group * pieces + part].astype(jnp.float32) for part in range(pieces)]
        for block in range(pieces):
            total = jnp.zeros((rows, LANES), jnp.float32)
            for part in range(pieces):
                shift = ((part - block) * own) % LANES
                moved = sources[part] if shift == 0 else pltpu.roll(sources[part], shift, 1)
                total = jnp.where(spot == part, moved, total)
            wide[block * rows : (block + 1) * rows, group * LANES : (group + 1) * LANES] = total


def pack(wide, packed, devices, own):
    pieces = LANES // own
    rows = packed.shape[1]
    spot = lax.broadcasted_iota(jnp.int32, (rows, LANES), 1) // own
    for group in range(devices // pieces):
        sources = [
            wide[block * rows : (block + 1) * rows, group * LANES : (group + 1) * LANES] for block in range(pieces)
        ]
        for part in range(pieces):
            total = jnp.zeros((rows, LANES), jnp.float32)
            for block in range(pieces):
                shift = ((block - part) * own) % LANES
                moved = sources[block] if shift == 0 else pltpu.roll(sources[block], shift, 1)
                total = jnp.where(spot == block, moved, total)
            packed[group * pieces + part] = total


def tap_sums(wide_dconv, wide_feat, terms, first, height, width, scale):
    chans = wide_feat.shape[2]

    @pl.loop(0, chans // LANES)
    def _(group):
        lanes = pl.ds(pl.multiple_of(group * LANES, LANES), LANES)
        for second in range(7):
            begin = LEFT - HALO + second
            total = jnp.zeros((width, LANES), jnp.float32)
            for row in range(height):
                total = total + (
                    wide_dconv[HALO + row, LEFT : LEFT + width, lanes]
                    * wide_feat[row + first, begin : begin + width, lanes]
                )
            tap = first * 7 + second
            terms[tap : tap + 1, lanes] = jnp.sum(total, axis=0, keepdims=True) * scale


def rows_at(step, most, height):
    return [row for row in range(height) if min(2, most) + row * (most - 1) // height == step]


def gather_kernel(
    ring, taps, up, down, small, feat,
    all_up, all_down, wide, rim, normed, normal_out, inv_out,
    all_small, wide_rows, conv,
    ring_out, ring_in, pair_out, pair_in, small_out, small_in, rim_out, rim_in, own_sem,
):
    devices = ring.devices
    me = lax.axis_index("row")
    core, chip = me % 2, me // 2
    partner = me + 1 - 2 * core
    place = ring.place(chip)
    mine, gathered = (up, down), (all_up, all_down)
    greet_all(me, devices)
    height, width, chans = feat.shape

    def normalise(row):
        def store(lanes, total):
            conv[:, lanes] = total + wide[taps : taps + 1, lanes]

        conv_row(wide_rows, wide, row, width, False, store)
        value = conv[...]
        centered = value - jnp.mean(value, axis=1, keepdims=True)
        inv = lax.rsqrt(jnp.mean(centered * centered, axis=1, keepdims=True) + eps)
        unit = centered * inv
        normed[row] = unit
        inv_out[row] = inv
        normal_out[row] = (unit * wide[taps + 1 : taps + 2, :] + wide[taps + 2 : taps + 3, :]).astype(normal_out.dtype)

    def lower_rim():
        return send(feat.at[pl.ds(height - HALO, HALO)], rim.at[0], rim_out.at[0], rim_in.at[0], lax.rem(me + 1, devices))

    def upper_rim():
        return send(feat.at[pl.ds(0, HALO)], rim.at[1], rim_out.at[1], rim_in.at[1], lax.rem(me + devices - 1, devices))

    @pl.when(me < devices - 1)
    def _():
        lower_rim().start()

    @pl.when(me > 0)
    def _():
        upper_rim().start()

    def small_copy(step):
        return send(small, all_small.at[me], small_out.at[step], small_in.at[step], lax.rem(me + step, devices))

    def small_arrival(step):
        source = lax.rem(me + devices - step, devices)
        return send(small, all_small.at[source], small_out.at[step], small_in.at[step], source)

    @pl.loop(1, devices)
    def _(step):
        small_copy(step).start()

    def owner(flow, step):
        return ring.chip_at(place - ring.flows[flow][0] * step) * 2 + core

    def hop(flow, step):
        direction, which, _ = ring.flows[flow]
        slot = owner(flow, step - 1)
        src = mine[which] if step == 1 else gathered[which].at[slot]
        target = ring.chip_at(place + direction) * 2 + core
        return send(src, gathered[which].at[slot], ring_out.at[flow, step - 1], ring_in.at[flow, step - 1], target)

    def hop_arrival(flow, step):
        direction, which, _ = ring.flows[flow]
        slot = owner(flow, step)
        source = ring.chip_at(place - direction) * 2 + core
        ref = gathered[which].at[slot]
        return send(ref, ref, ring_out.at[flow, step - 1], ring_in.at[flow, step - 1], source)

    def hand(flow, step):
        which = ring.flows[flow][1]
        slot = me if step == 0 else owner(flow, step)
        src = mine[which] if step == 0 else gathered[which].at[slot]
        return send(src, gathered[which].at[slot], pair_out.at[flow, step], pair_in.at[flow, step], partner)

    def hand_arrival(flow, step):
        which = ring.flows[flow][1]
        slot = (partner if step == 0 else ring.chip_at(place - ring.flows[flow][0] * step) * 2 + 1 - core)
        ref = gathered[which].at[slot]
        return send(ref, ref, pair_out.at[flow, step], pair_in.at[flow, step], partner)

    flows = range(len(ring.flows))
    for step in range(1, ring.most + 1):
        for flow in flows:
            hops = ring.flows[flow][2]
            if step <= hops:
                if step > 1:
                    hop_arrival(flow, step - 1).wait_recv()
                hop(flow, step).start()
                if step > 1:
                    hand(flow, step - 1).start()
        if step == 1:
            for flow in (0, 1):
                hand(flow, 0).start()
            fill_middle(wide_rows, feat)
            owns = [
                pltpu.make_async_copy(up, all_up.at[me], own_sem.at[0]),
                pltpu.make_async_copy(down, all_down.at[me], own_sem.at[1]),
                pltpu.make_async_copy(small, all_small.at[me], own_sem.at[2]),
            ]
            for own in owns:
                own.start()

            @pl.when(me == 0)
            def _():
                rim[0] = jnp.zeros(rim.shape[1:], rim.dtype)

            @pl.when(me == devices - 1)
            def _():
                rim[1] = jnp.zeros(rim.shape[1:], rim.dtype)

            owns[2].wait()

            @pl.loop(1, devices)
            def _(other):
                small_arrival(other).wait_recv()

            unpack(all_small, wide, devices, chans // devices)

            @pl.when(me < devices - 1)
            def _():
                upper_rim().wait_recv()

            @pl.when(me > 0)
            def _():
                lower_rim().wait_recv()

            fill_rims(wide_rows, rim, height, width)
        for row in rows_at(step, ring.most, height):
            normalise(row)

    for flow in flows:
        hops = ring.flows[flow][2]
        hop_arrival(flow, hops).wait_recv()
        hand(flow, hops).start()
    for flow in flows:
        hops = ring.flows[flow][2]
        for step in range(0 if flow < 2 else 1, hops + 1):
            hand_arrival(flow, step).wait_recv()
            hand(flow, step).wait_send()
        for step in range(1, hops + 1):
            hop(flow, step).wait_send()

    @pl.loop(1, devices)
    def _(step):
        small_copy(step).wait_send()

    for own in owns[:2]:
        own.wait()

    @pl.when(me < devices - 1)
    def _():
        lower_rim().wait_send()

    @pl.when(me > 0)
    def _():
        upper_rim().wait_send()


def scatter_kernel(
    ring, scale, up, down, rest, dconv, wide, cot, feat, feat_rim,
    own_up, own_down, own_small, grad_feat,
    half_up, half_down, got_up, got_down, out_up, out_down, got_small, rim, wide_rows, wide_feat, terms, small,
    ring_out, ring_in, pair_out, pair_in, small_out, small_in, rim_out, rim_in,
):
    devices = ring.devices
    me = lax.axis_index("row")
    core, chip = me % 2, me // 2
    partner = me + 1 - 2 * core
    place = ring.place(chip)
    parts, halves = (up, down), (half_up, half_down)
    got, out, total = (got_up, got_down), (out_up, out_down), (own_up, own_down)
    greet_all(me, devices)

    height, width, _ = dconv.shape

    def lower_rim():
        return send(dconv.at[pl.ds(height - HALO, HALO)], rim.at[0], rim_out.at[0], rim_in.at[0], lax.rem(me + 1, devices))

    def upper_rim():
        return send(dconv.at[pl.ds(0, HALO)], rim.at[1], rim_out.at[1], rim_in.at[1], lax.rem(me + devices - 1, devices))

    def spread(row):
        def store(lanes, total):
            grad_feat[row, :, lanes] = (cot[row, :, lanes].astype(jnp.float32) + total).astype(grad_feat.dtype)

        conv_row(wide_rows, wide, row, width, True, store)

    def pair(which, offset):
        slot = ring.chip_at(place + offset)
        return send(
            parts[which].at[slot, 1 - core], halves[which].at[offset],
            pair_out.at[which, offset], pair_in.at[which, offset], partner,
        )

    half = ring.chips // 2
    order = [half]
    for near in range(half - 1, 0, -1):
        order += [near, ring.chips - near]
    order.append(0)
    for offset in order:
        for which in (0, 1):
            pair(which, offset).start()

    @pl.when(me < devices - 1)
    def _():
        lower_rim().start()

    @pl.when(me > 0)
    def _():
        upper_rim().start()

    def small_copy(step):
        target = lax.rem(me + step, devices)
        return send(small.at[target], got_small.at[step], small_out.at[step], small_in.at[step], target)

    def hop(flow, step):
        direction, which, _ = ring.flows[flow]
        side = 0 if direction > 0 else 1
        target = ring.chip_at(place + direction) * 2 + core
        return send(
            out[which].at[side, step - 1], got[which].at[side, step - 1],
            ring_out.at[flow, step - 1], ring_in.at[flow, step - 1], target,
        )

    known = set()

    def chip_sum(which, offset):
        offset = offset % ring.chips
        if (which, offset) not in known:
            pair(which, offset).wait_recv()
            known.add((which, offset))
        slot = ring.chip_at(place + offset)
        return parts[which][slot, core].astype(jnp.float32) + halves[which][offset].astype(jnp.float32)

    flows = range(len(ring.flows))
    for step in range(1, ring.most + 1):
        for flow in flows:
            direction, which, hops = ring.flows[flow]
            side = 0 if direction > 0 else 1
            if step <= hops:
                value = chip_sum(which, direction * (hops - step + 1))
                if step > 1:
                    hop(flow, step - 1).wait_recv()
                    value = value + got[which][side, step - 2].astype(jnp.float32)
                out[which][side, step - 1] = value.astype(out[which].dtype)
                hop(flow, step).start()
        if step == 1:
            fill_middle(wide_rows, dconv)

            @pl.when(me == 0)
            def _():
                rim[0] = jnp.zeros(rim.shape[1:], rim.dtype)

            @pl.when(me == devices - 1)
            def _():
                rim[1] = jnp.zeros(rim.shape[1:], rim.dtype)

            @pl.when(me < devices - 1)
            def _():
                upper_rim().wait_recv()

            @pl.when(me > 0)
            def _():
                lower_rim().wait_recv()

            fill_rims(wide_rows, rim, height, width)
            fill_middle(wide_feat, feat)
            fill_rims(wide_feat, feat_rim, height, width)
            terms[...] = rest[...]
        for first in range(7):
            if first * ring.most // 7 + 1 == step:
                tap_sums(wide_rows, wide_feat, terms, first, height, width, scale)
        if step == ring.most:
            pack(terms, small, devices, terms.shape[1] // devices)

            @pl.loop(1, devices)
            def _(other):
                small_copy(other).start()

        for row in rows_at(step, ring.most, height):
            spread(row)

    step_sum = small[me]
    for step in range(1, devices):
        small_copy(step).wait_recv()
        step_sum = step_sum + got_small[step]
    own_small[...] = step_sum
    for which in (0, 1):
        value = chip_sum(which, 0)
        for flow in flows:
            direction, flow_which, hops = ring.flows[flow]
            side = 0 if direction > 0 else 1
            if flow_which == which:
                hop(flow, hops).wait_recv()
                value = value + got[which][side, hops - 1].astype(jnp.float32)
        total[which][...] = value

    for offset in order:
        for which in (0, 1):
            pair(which, offset).wait_send()
    for flow in flows:
        for step in range(1, ring.flows[flow][2] + 1):
            hop(flow, step).wait_send()

    @pl.loop(1, devices)
    def _(step):
        small_copy(step).wait_send()

    @pl.when(me < devices - 1)
    def _():
        lower_rim().wait_send()

    @pl.when(me > 0)
    def _():
        upper_rim().wait_send()


def vmem():
    return pl.BlockSpec(memory_space=pltpu.VMEM)


def gather(ring, taps, filled, up, down, small, feat):
    height, width, chans = feat.shape
    devices, most, flows = ring.devices, ring.most, len(ring.flows)
    dma = pltpu.SemaphoreType.DMA
    return pl.pallas_call(
        functools.partial(gather_kernel, ring, taps),
        out_shape=(
            jax.ShapeDtypeStruct((devices,) + up.shape, up.dtype),
            jax.ShapeDtypeStruct((devices,) + down.shape, down.dtype),
            jax.ShapeDtypeStruct((filled, chans), jnp.float32),
            jax.ShapeDtypeStruct((2, HALO) + feat.shape[1:], feat.dtype),
            jax.ShapeDtypeStruct(feat.shape, jnp.float32),
            jax.ShapeDtypeStruct(feat.shape, jnp.bfloat16),
            jax.ShapeDtypeStruct((height, width, 1), jnp.float32),
        ),
        in_specs=[vmem()] * 4,
        out_specs=(vmem(),) * 7,
        scratch_shapes=[
            pltpu.VMEM((devices,) + small.shape, small.dtype),
            pltpu.VMEM((height + 2 * HALO, width + 2 * LEFT, chans), jnp.float32),
            pltpu.VMEM((width, chans), jnp.float32),
            dma((flows, most)), dma((flows, most)),
            dma((flows, most + 1)), dma((flows, most + 1)),
            dma((devices,)), dma((devices,)),
            dma((2,)), dma((2,)), dma((3,)),
        ],
        compiler_params=pltpu.CompilerParams(
            collective_id=0, has_side_effects=True, vmem_limit_bytes=56 * 2**20
        ),
        name="gather",
    )(up, down, small, feat)


def scatter(ring, scale, up, down, rest, dconv, wide, cot, feat, feat_rim):
    height, width, chans = dconv.shape
    devices, most, flows, chips = ring.devices, ring.most, len(ring.flows), ring.chips
    dma = pltpu.SemaphoreType.DMA
    block_up, block_down = up.shape[2:], down.shape[2:]
    kind = up.dtype
    packed = (devices, rest.shape[0] * rest.shape[1] // devices // LANES, LANES)
    return pl.pallas_call(
        functools.partial(scatter_kernel, ring, scale),
        out_shape=(
            jax.ShapeDtypeStruct(block_up, jnp.float32),
            jax.ShapeDtypeStruct(block_down, jnp.float32),
            jax.ShapeDtypeStruct(packed[1:], jnp.float32),
            jax.ShapeDtypeStruct(cot.shape, cot.dtype),
        ),
        in_specs=[vmem()] * 8,
        out_specs=(vmem(),) * 4,
        scratch_shapes=[
            pltpu.VMEM((chips,) + block_up, kind),
            pltpu.VMEM((chips,) + block_down, kind),
            pltpu.VMEM((2, most) + block_up, kind),
            pltpu.VMEM((2, most) + block_down, kind),
            pltpu.VMEM((2, most) + block_up, kind),
            pltpu.VMEM((2, most) + block_down, kind),
            pltpu.VMEM(packed, jnp.float32),
            pltpu.VMEM((2, HALO, width, chans), dconv.dtype),
            pltpu.VMEM((height + 2 * HALO, width + 2 * LEFT, chans), jnp.float32),
            pltpu.VMEM((height + 2 * HALO, width + 2 * LEFT, chans), jnp.float32),
            pltpu.VMEM(rest.shape, jnp.float32),
            pltpu.VMEM(packed, jnp.float32),
            dma((flows, most)), dma((flows, most)),
            dma((2, chips)), dma((2, chips)),
            dma((devices,)), dma((devices,)),
            dma((2,)), dma((2,)),
        ],
        compiler_params=pltpu.CompilerParams(
            collective_id=1, has_side_effects=True, vmem_limit_bytes=56 * 2**20
        ),
        name="scatter",
    )(up, down, rest, dconv, wide, cot, feat, feat_rim)


def gelu_parts(value):
    cumulative = 0.5 * (1.0 + lax.erf(value * (1.0 / math.sqrt(2.0))))
    density = jnp.exp(-0.5 * value * value) * (1.0 / math.sqrt(2.0 * math.pi))
    return value * cumulative, cumulative + value * density


def per_device(
    ring,
    features,
    cotangent,
    depth_weight,
    depth_bias,
    norm_gain,
    norm_shift,
    up_weight,
    up_bias,
    down_weight,
    down_bias,
):
    height, width, chans = features.shape
    devices = ring.devices
    cells = height * width
    own = chans // devices
    units = up_weight.shape[1]
    ratio = units // chans
    scale = 1.0 / math.sqrt(cells * devices)
    packed = jnp.concatenate(
        [depth_weight, depth_bias[None], norm_gain[None], norm_shift[None], down_bias[None], up_bias.reshape(ratio, own)],
        axis=0,
    )
    rows = packed.shape[0]
    filled = -(-rows // 64) * 64
    pieces = LANES // own
    packed = jnp.pad(packed, ((0, filled - rows), (0, 0)))
    packed = packed.reshape(pieces, filled // pieces, own).transpose(1, 0, 2).reshape(filled // pieces, LANES)
    taps = depth_weight.shape[0]
    all_up, all_down, wide, rim, normed, normal_out, inv = gather(
        ring, taps, filled, up_weight, down_weight, packed, features
    )
    up_full = all_up.reshape(chans, units)
    down_full = all_down.reshape(units, chans)
    gain, bias_down = wide[taps + 1], wide[taps + 3]
    bias_up = wide[taps + 4 : taps + 4 + ratio].reshape(ratio, devices, own).transpose(1, 0, 2).reshape(units)
    flat_norm = normal_out.reshape(cells, chans)
    flat_cot = cotangent.reshape(cells, chans)
    hidden = jnp.dot(flat_norm, up_full, preferred_element_type=jnp.float32) + bias_up
    act, slope = gelu_parts(hidden)
    act = act.astype(jnp.bfloat16)
    mixed = jnp.dot(act, down_full, preferred_element_type=jnp.float32)
    block_out = (features.astype(jnp.float32) + (mixed + bias_down).reshape(height, width, chans)).astype(jnp.bfloat16)
    kind = jnp.bfloat16
    down_part = (
        lax.dot_general(act, flat_cot, (((0,), (0,)), ((), ())), preferred_element_type=jnp.float32) * scale
    ).astype(kind)
    dact = lax.dot_general(flat_cot, down_full, (((1,), (1,)), ((), ())), preferred_element_type=jnp.float32)
    dhidden = (dact * slope).astype(jnp.bfloat16)
    up_part = (
        lax.dot_general(flat_norm, dhidden, (((0,), (0,)), ((), ())), preferred_element_type=jnp.float32) * scale
    ).astype(kind)
    dnorm = lax.dot_general(dhidden, up_full, (((1,), (1,)), ((), ())), preferred_element_type=jnp.float32)
    dnorm = dnorm.reshape(height, width, chans)
    down_bias_term = jnp.sum(flat_cot.astype(jnp.float32), axis=0)
    up_bias_term = jnp.sum(dhidden.astype(jnp.float32), axis=0)
    gain_term = jnp.sum(dnorm * normed, axis=(0, 1))
    shift_term = jnp.sum(dnorm, axis=(0, 1))
    scaled = dnorm * gain
    dconv = inv * (
        scaled
        - jnp.mean(scaled, axis=2, keepdims=True)
        - normed * jnp.mean(scaled * normed, axis=2, keepdims=True)
    )
    dconv = dconv.astype(jnp.bfloat16)
    dconv_wide = dconv.astype(jnp.float32)
    conv_bias_term = jnp.sum(dconv_wide, axis=(0, 1))
    terms = jnp.concatenate(
        [
            jnp.zeros((taps, chans), jnp.float32),
            jnp.stack([conv_bias_term, gain_term, shift_term, down_bias_term], axis=0),
            up_bias_term.reshape(devices, ratio, own).transpose(1, 0, 2).reshape(ratio, chans),
        ],
        axis=0,
    ) * scale
    terms = jnp.pad(terms, ((0, filled - rows), (0, 0)))
    grad_up, grad_down, own_terms, grad_features = scatter(
        ring,
        scale,
        up_part.reshape(ring.chips, 2, chans // devices, units),
        down_part.reshape(ring.chips, 2, units // devices, chans),
        terms,
        dconv,
        wide,
        cotangent,
        features,
        rim,
    )
    own_terms = own_terms.reshape(filled // pieces, pieces, own).transpose(1, 0, 2).reshape(filled, own)
    return (
        block_out,
        grad_features,
        grad_up,
        grad_down,
        own_terms[:taps],
        own_terms[taps],
        own_terms[taps + 1],
        own_terms[taps + 2],
        own_terms[taps + 4 : taps + 4 + ratio].reshape(ratio * own),
        own_terms[taps + 3],
    )


def solution(mesh):
    ring = Ring(mesh.shape["row"], fold_of(mesh))
    placed = (
        P(("groups", "row"), None, None),
        P(("groups", "row"), None, None),
        P(None, "row"),
        P("row"),
        P("row"),
        P("row"),
        P("row", None),
        P("row"),
        P("row", None),
        P("row"),
    )
    return jax.shard_map(
        functools.partial(per_device, ring),
        mesh=mesh,
        in_specs=placed,
        out_specs=(
            P(("groups", "row"), None, None),
            P(("groups", "row"), None, None),
            P(("groups", "row"), None),
            P(("groups", "row"), None),
            P("groups", "row"),
            P(("groups", "row")),
            P(("groups", "row")),
            P(("groups", "row")),
            P(("groups", "row")),
            P(("groups", "row")),
        ),
        check_vma=False,
    )
```
